32 devices in a mesh: pipe: 4 (over y, x), dp: 8 (over z, core).
Axes of the slice: x: 2, y: 2, z: 4, core: 2. Of those that a mesh axis runs over, the one named last changes fastest.
Arguments:
- inputs: bfloat16 [6, 256, 8192], P(None, 'dp'), may hold values from -6 to 6
- cotangent: bfloat16 [6, 256, 8192], P(None, 'dp'), may hold values from -0.19921875 to 0.19921875
- plan_order: int32 [6], replicated, may hold values from 0 to 5, each once
- norm_gain: float32 [4, 8192], P('pipe'), may hold values from 0.5 to 1.5
- weight_in: bfloat16 [4, 8192, 512], P('pipe'), may hold values from -0.0625 to 0.0625
- weight_out: bfloat16 [4, 512, 8192], P('pipe'), may hold values from -0.25 to 0.25
Outputs:
- grad_in: bfloat16 [4, 8192, 512], P('pipe', 'dp')
- grad_out: bfloat16 [4, 512, 8192], P('pipe', None, 'dp')
The draws below stay inside these ranges and needn't reach their ends.
Inputs may be any that keep to these rules, and one draw needn't show every extreme that they name: plan_order names each slot's sample once: a permutation.
All inputs are finite; a program needn't handle non-finite values.
Results may differ from the reference program's by a relative error of at most 0.024.
Values may be sent and summed in bfloat16 or wider, within the bound.
A program may use at most 128 MiB of HBM per device.

```python
import jax
import jax.numpy as jnp
from jax import lax

D = 8192
R = 512
MICRO = 6
ROWS = 256
SECTIONS = 4
N_DP = 8


def raised(entries, own_key, source, target, parts, factor):
    def block_of(position):
        return (jnp.arange(entries.shape[position]) // (entries.shape[position] // parts)).reshape((-1,) + (1,) * (entries.ndim - 1 - position))

    near = jax.random.permutation(own_key, parts)[block_of(target)]
    far = (block_of(target) + parts // 2) % parts
    return jnp.where((block_of(source) == near) | (block_of(source) == far), factor * entries, entries)


def level_of(key, dims, cuts, low, top_value):
    gain = 1.0
    for dim, blocks in cuts:
        draws = jax.random.uniform(jax.random.fold_in(jax.random.fold_in(key, 6), dim), (blocks,), jnp.float32, low / len(cuts), top_value / len(cuts))
        gain = gain * jnp.repeat(jnp.exp(draws), dims[dim] // blocks).reshape((-1,) + (1,) * (len(dims) - 1 - dim))
    return gain


def bell_draw(key, dims, deviation, most, cuts=(), kind=jnp.bfloat16):
    factor_of = level_of(key, dims, cuts, -0.22, 0.18) if cuts else 1.0
    entries = jax.random.normal(key, dims, jnp.float32) * deviation * factor_of
    return jnp.minimum(jnp.maximum(entries, -most), most).astype(kind)


def bell_draw_with(own_key, shape, deviation, reach, cuts, heavy, held_as=jnp.bfloat16):
    values = deviation * jax.random.normal(own_key, shape, jnp.float32)
    if cuts:
        values = values * level_of(own_key, shape, cuts, -0.22, 0.18)
    return jnp.clip(raised(values, jax.random.fold_in(own_key, 3), *heavy), -reach, reach).astype(held_as)


def setup_inputs(seed: int = 0) -> dict:
    keys = jax.random.split(jax.random.key(seed), 7)
    return {
        "inputs": bell_draw_with(keys[0], (MICRO, ROWS, D), 1.0, 6.0, ((1, 8),), (1, 2, 8, 2.0)),
        "cotangent": bell_draw_with(keys[1], (MICRO, ROWS, D), 0.03, 0.19921875, ((1, 8),), (1, 2, 8, 2.0)),
        "plan_order": jax.random.permutation(keys[2], MICRO).astype(jnp.int32),
        "norm_gain": jnp.clip(1.0 + 0.1 * jax.random.normal(keys[3], (SECTIONS, D), jnp.float32), 0.5, 1.5),
        "weight_in": bell_draw(keys[4], (SECTIONS, D, R), D ** -0.5, 0.0625, ((0, 4),)),
        "weight_out": bell_draw(keys[5], (SECTIONS, R, D), R ** -0.5, 0.25, ((0, 4),)),
    }


EPSILON = 1e-05

def inner_section(rows_in, gain_row, weight_first):
    float_cast = rows_in.astype(jnp.float32)
    inverse_root_mean = lax.rsqrt(lax.optimization_barrier(jnp.mean(float_cast * float_cast, axis=-1, keepdims=True)) + EPSILON)
    normed = (float_cast * inverse_root_mean * gain_row).astype(jnp.bfloat16)
    pre_act = jnp.dot(normed, weight_first, preferred_element_type=jnp.float32)
    hidden = jax.nn.silu(pre_act).astype(jnp.bfloat16)
    return (float_cast, inverse_root_mean, normed, pre_act, hidden)

def reference(inputs, cotangent, plan_order, norm_gain, weight_in, weight_out):
    section_count = norm_gain.shape[0]
    micro_count, row_count, model_width = inputs.shape
    inner_width = weight_in.shape[2]
    rows_now = inputs[plan_order.astype(jnp.int32)].reshape(micro_count * row_count, model_width)
    saved = []
    for section_index in range(section_count):
        saved.append(rows_now)
        float_cast, inverse_root_mean, normed, pre_act, hidden = inner_section(rows_now, norm_gain[section_index], weight_in[section_index])
        rows_now = (float_cast + jnp.dot(hidden, weight_out[section_index], preferred_element_type=jnp.float32)).astype(jnp.bfloat16)

    def split_dp(array):
        last = array.shape[-1]
        grouped = array.reshape(micro_count, N_DP, row_count // N_DP, last)
        return jnp.transpose(grouped, (1, 0, 2, 3)).reshape(N_DP, -1, last)

    def add_source(totals, items):
        normed_q, grad_q, hidden_q, up_q = items
        term_in = jnp.dot(normed_q.T, grad_q, preferred_element_type=jnp.float32)
        term_out = jnp.dot(hidden_q.T, up_q, preferred_element_type=jnp.float32)
        term_in = lax.optimization_barrier(term_in.astype(jnp.bfloat16)).astype(jnp.float32)
        term_out = lax.optimization_barrier(term_out.astype(jnp.bfloat16)).astype(jnp.float32)
        return ((totals[0] + term_in, totals[1] + term_out), None)
    incoming_gradient = cotangent.reshape(micro_count * row_count, model_width)
    grads_first = [None] * section_count
    grads_second = [None] * section_count
    for section_index in reversed(range(section_count)):
        gain_row = norm_gain[section_index]
        float_cast, inverse_root_mean, normed, pre_act, hidden = inner_section(saved[section_index], gain_row, weight_in[section_index])
        grad_hidden = jnp.dot(incoming_gradient, weight_out[section_index].T, preferred_element_type=jnp.float32)
        sigmoid_pre = jax.nn.sigmoid(pre_act)
        grad_pre = (grad_hidden * sigmoid_pre * (1.0 + pre_act * (1.0 - sigmoid_pre))).astype(jnp.bfloat16)
        back_rows = jnp.dot(grad_pre, weight_in[section_index].T, preferred_element_type=jnp.float32)
        zeros_in = jnp.zeros((model_width, inner_width), jnp.float32)
        zeros_out = jnp.zeros((inner_width, model_width), jnp.float32)
        (total_in, total_out), unused = lax.scan(add_source, (zeros_in, zeros_out), (split_dp(normed), split_dp(grad_pre), split_dp(hidden), split_dp(incoming_gradient)))
        grads_first[section_index] = total_in.astype(jnp.bfloat16)
        grads_second[section_index] = total_out.astype(jnp.bfloat16)
        normalized_input = float_cast * inverse_root_mean
        rescaled_rows = back_rows * gain_row
        incoming_gradient = (incoming_gradient.astype(jnp.float32) + inverse_root_mean * (rescaled_rows - normalized_input * lax.optimization_barrier(jnp.mean(rescaled_rows * normalized_input, axis=-1, keepdims=True)))).astype(jnp.bfloat16)
    return (jnp.stack(grads_first), jnp.stack(grads_second))
```

```python
import functools

import jax
import jax.numpy as jnp
from jax import lax
from jax.experimental import pallas as pl
from jax.experimental.pallas import tpu as pltpu
from jax.sharding import PartitionSpec as P

EPSILON = 1e-05
MESH = pl.DeviceIdType.MESH
CHUNK = 1024
UNROLL = 2


def landed(ref, sem):
    pltpu.make_async_copy(ref, ref, sem).wait()


def train_kernel(
    sections,
    peers,
    rows_hbm,
    cot_hbm,
    gain,
    w_in,
    w_out,
    normed_all,
    up_all,
    hidden_all,
    grad_all,
    xbuf,
    ubuf,
    xsend,
    usend,
    normed,
    back,
    pre_kept,
    hidden_kept,
    grad_kept,
    inv_kept,
    x_recv,
    u_recv,
    x_sent,
    u_sent,
    n_sems,
    p_sems,
    h_sems,
    g_sems,
):
    stage = lax.axis_index("pipe")
    me = lax.axis_index("dp")
    last = sections - 1
    micro, rows, width = xbuf.shape
    share = width // peers
    chunk = min(CHUNK, width)
    chunks = width // chunk

    barrier = pltpu.get_barrier_semaphore()
    for j in range(1, peers):
        pl.semaphore_signal(
            barrier, inc=1, device_id={"dp": lax.rem(me + j, peers)}, device_id_type=MESH
        )

    @pl.when(stage < last)
    def _():
        pl.semaphore_signal(barrier, inc=1, device_id={"pipe": stage + 1}, device_id_type=MESH)

    @pl.when(stage > 0)
    def _():
        pl.semaphore_signal(barrier, inc=1, device_id={"pipe": stage - 1}, device_id_type=MESH)

    pl.semaphore_wait(
        barrier, peers - 1 + jnp.minimum(stage, 1) + jnp.minimum(last - stage, 1)
    )

    @pl.when(stage == 0)
    def _():
        for m in range(micro):
            pltpu.make_async_copy(rows_hbm.at[m], xbuf.at[m], x_recv.at[m]).start()

    @pl.when(stage == last)
    def _():
        for m in range(micro):
            pltpu.make_async_copy(cot_hbm.at[m], ubuf.at[m], u_recv.at[m]).start()

    def cols(c):
        return pl.ds(pl.multiple_of(c * chunk, chunk), chunk)

    def spread_columns(source, target, sems, m):
        for j in range(1, peers):
            peer = lax.rem(me + j, peers)
            pltpu.make_async_remote_copy(
                src_ref=source.at[m, :, pl.ds(pl.multiple_of(peer * share, share), share)],
                dst_ref=target.at[me, m],
                send_sem=sems.at[0],
                recv_sem=sems.at[1],
                device_id={"dp": peer},
                device_id_type=MESH,
            ).start()
        pltpu.make_async_copy(
            source.at[m, :, pl.ds(pl.multiple_of(me * share, share), share)],
            target.at[me, m],
            sems.at[1],
        ).start()

    def spread_whole(source, target, sems, m):
        for j in range(1, peers):
            pltpu.make_async_remote_copy(
                src_ref=source.at[m],
                dst_ref=target.at[me, m],
                send_sem=sems.at[0],
                recv_sem=sems.at[1],
                device_id={"dp": lax.rem(me + j, peers)},
                device_id_type=MESH,
            ).start()
        pltpu.make_async_copy(source.at[m], target.at[me, m], sems.at[1]).start()

    def pass_on(source, target, send, recv, m, to):
        return pltpu.make_async_remote_copy(
            src_ref=source.at[m],
            dst_ref=target.at[m],
            send_sem=send.at[m],
            recv_sem=recv.at[m],
            device_id={"pipe": to},
            device_id_type=MESH,
        )

    def forward(m):
        landed(xbuf.at[m], x_recv.at[m])

        def square(c, total):
            x = xbuf[m, :, cols(c)].astype(jnp.float32)
            return total + jnp.sum(x * x, axis=-1, keepdims=True)

        total = lax.fori_loop(
            0, chunks, square, jnp.zeros((rows, 1), jnp.float32), unroll=UNROLL
        )
        inverse = lax.rsqrt(total / width + EPSILON)
        inv_kept[m] = jnp.broadcast_to(inverse, inv_kept.shape[1:])

        def project(c, pre):
            x = xbuf[m, :, cols(c)].astype(jnp.float32)
            n = (x * inverse * gain[:, cols(c)]).astype(jnp.bfloat16)
            normed[m, :, cols(c)] = n
            return pre + jnp.dot(n, w_in[cols(c), :], preferred_element_type=jnp.float32)

        pre = lax.fori_loop(
            0, chunks, project, jnp.zeros((rows, w_in.shape[1]), jnp.float32), unroll=UNROLL
        )
        pre_kept[m] = pre
        hidden = jax.nn.silu(pre).astype(jnp.bfloat16)
        hidden_kept[m] = hidden

        @pl.when(stage < last)
        def _():
            def emit(c, carry):
                x = xbuf[m, :, cols(c)].astype(jnp.float32)
                y = jnp.dot(hidden, w_out[:, cols(c)], preferred_element_type=jnp.float32)
                xsend[m, :, cols(c)] = (x + y).astype(jnp.bfloat16)
                return carry

            lax.fori_loop(0, chunks, emit, 0, unroll=UNROLL)
            pass_on(xsend, xbuf, x_sent, x_recv, m, stage + 1).start()

        spread_columns(normed, normed_all, n_sems, m)
        spread_whole(hidden_kept, hidden_all, h_sems, m)

    def backward(m):
        landed(ubuf.at[m], u_recv.at[m])
        contract = (((1,), (1,)), ((), ()))

        def collect(c, total):
            return total + lax.dot_general(
                ubuf[m, :, cols(c)],
                w_out[:, cols(c)],
                contract,
                preferred_element_type=jnp.float32,
            )

        grad_hidden = lax.fori_loop(
            0, chunks, collect, jnp.zeros((rows, w_in.shape[1]), jnp.float32), unroll=UNROLL
        )
        pre = pre_kept[m]
        sig = jax.nn.sigmoid(pre)
        grad_pre = (grad_hidden * sig * (1.0 + pre * (1.0 - sig))).astype(jnp.bfloat16)
        grad_kept[m] = grad_pre

        @pl.when(stage > 0)
        def _():
            inverse = inv_kept[m][:, :1]

            def scale(c, total):
                t = lax.dot_general(
                    grad_pre, w_in[cols(c), :], contract, preferred_element_type=jnp.float32
                )
                t = t * gain[:, cols(c)]
                back[:, cols(c)] = t
                xhat = xbuf[m, :, cols(c)].astype(jnp.float32) * inverse
                return total + jnp.sum(t * xhat, axis=-1, keepdims=True)

            total = lax.fori_loop(
                0, chunks, scale, jnp.zeros((rows, 1), jnp.float32), unroll=UNROLL
            )
            mean = total / width

            def emit(c, carry):
                xhat = xbuf[m, :, cols(c)].astype(jnp.float32) * inverse
                u = ubuf[m, :, cols(c)].astype(jnp.float32)
                usend[m, :, cols(c)] = (
                    u + inverse * (back[:, cols(c)] - xhat * mean)
                ).astype(jnp.bfloat16)
                return carry

            lax.fori_loop(0, chunks, emit, 0, unroll=UNROLL)
            pass_on(usend, ubuf, u_sent, u_recv, m, stage - 1).start()

        spread_columns(ubuf, up_all, p_sems, m)
        spread_whole(grad_kept, grad_all, g_sems, m)

    delay = jnp.minimum(2 * (last - stage), micro)

    def step(k, carry):
        @pl.when(k < micro)
        def _():
            forward(k)

        @pl.when((k >= delay) & (k < delay + micro))
        def _():
            backward(k - delay)

        return carry

    lax.fori_loop(0, micro + min(2 * last, micro), step, 0)

    for m in range(micro):

        @pl.when(stage < last)
        def _(m=m):
            pass_on(xsend, xbuf, x_sent, x_recv, m, stage + 1).wait_send()

        @pl.when(stage > 0)
        def _(m=m):
            pass_on(usend, ubuf, u_sent, u_recv, m, stage - 1).wait_send()

    if peers > 1:
        landed(normed_all.at[pl.ds(0, peers - 1)], n_sems.at[0])
        landed(up_all.at[pl.ds(0, peers - 1)], p_sems.at[0])
        landed(hidden_all.at[pl.ds(0, peers - 1)], h_sems.at[0])
        landed(grad_all.at[pl.ds(0, peers - 1)], g_sems.at[0])
    landed(normed_all, n_sems.at[1])
    landed(up_all, p_sems.at[1])
    landed(hidden_all, h_sems.at[1])
    landed(grad_all, g_sems.at[1])


def per_device(sections, peers, inputs, cotangent, plan_order, norm_gain, weight_in, weight_out):
    micro, rows, width = inputs.shape
    inner = weight_in.shape[2]
    share = width // peers
    ordered = jnp.take(inputs, plan_order, axis=0, mode="clip")
    wide, narrow = (micro, rows, width), (micro, rows, inner)
    half, full = jnp.bfloat16, jnp.float32
    dma = pltpu.SemaphoreType.DMA
    anywhere = pl.BlockSpec(memory_space=pl.ANY)
    local = pl.BlockSpec(memory_space=pltpu.VMEM)
    normed_all, up_all, hidden_all, grad_all = pl.pallas_call(
        functools.partial(train_kernel, sections, peers),
        out_shape=(
            jax.ShapeDtypeStruct((peers, micro, rows, share), half),
            jax.ShapeDtypeStruct((peers, micro, rows, share), half),
            jax.ShapeDtypeStruct((peers, micro, rows, inner), half),
            jax.ShapeDtypeStruct((peers, micro, rows, inner), half),
        ),
        in_specs=[anywhere, anywhere, local, local, local],
        out_specs=[anywhere] * 4,
        scratch_shapes=[pltpu.VMEM(wide, half)] * 5
        + [
            pltpu.VMEM((rows, width), full),
            pltpu.VMEM(narrow, full),
            pltpu.VMEM(narrow, half),
            pltpu.VMEM(narrow, half),
            pltpu.VMEM((micro, rows, 128), full),
        ]
        + [dma((micro,))] * 4
        + [dma((2,))] * 4,
        compiler_params=pltpu.CompilerParams(
            collective_id=0, has_side_effects=True, vmem_limit_bytes=60 * 1024 * 1024
        ),
    )(ordered, cotangent, norm_gain, weight_in[0], weight_out[0])
    tokens = peers * micro * rows
    total_in = jnp.einsum(
        "td,tr->dr",
        normed_all.reshape(tokens, share),
        grad_all.reshape(tokens, inner),
        preferred_element_type=full,
    )
    total_out = jnp.einsum(
        "tr,td->rd",
        hidden_all.reshape(tokens, inner),
        up_all.reshape(tokens, share),
        preferred_element_type=full,
    )
    return (total_in.astype(half)[None], total_out.astype(half)[None])


def solution(mesh):
    in_specs = (
        P(None, "dp", None),
        P(None, "dp", None),
        P(),
        P("pipe", None),
        P("pipe", None, None),
        P("pipe", None, None),
    )
    out_specs = (P("pipe", "dp", None), P("pipe", None, "dp"))
    return jax.shard_map(
        functools.partial(per_device, mesh.shape["pipe"], mesh.shape["dp"]),
        mesh=mesh,
        in_specs=in_specs,
        out_specs=out_specs,
        check_vma=False,
    )
```

```python
import functools

import jax
import jax.numpy as jnp
from jax import lax
from jax.experimental import pallas as pl
from jax.experimental.pallas import tpu as pltpu
from jax.sharding import PartitionSpec as P

EPSILON = 1e-05
MESH = pl.DeviceIdType.MESH
CHUNK = 1024
UNROLL = 8
PIECES = 4


def landed(ref, sem):
    pltpu.make_async_copy(ref, ref, sem).wait()


def train_kernel(
    sections,
    peers,
    rows_hbm,
    cot_hbm,
    gain,
    w_in,
    w_out,
    normed_all,
    up_all,
    hidden_all,
    grad_all,
    xbuf,
    ubuf,
    xsend,
    usend,
    normed,
    pre_kept,
    hidden_kept,
    grad_kept,
    inv_kept,
    x_recv,
    u_recv,
    x_sent,
    u_sent,
    n_sems,
    p_sems,
    h_sems,
    g_sems,
):
    stage = lax.axis_index("pipe")
    me = lax.axis_index("dp")
    last = sections - 1
    micro, rows, width = xbuf.shape
    share = width // peers
    chunk = min(CHUNK, width)
    chunks = width // chunk
    piece = width // PIECES
    pieces = [pl.ds(p * piece, piece) for p in range(PIECES)]
    per_piece = chunks // PIECES

    barrier = pltpu.get_barrier_semaphore()
    for j in range(1, peers):
        pl.semaphore_signal(
            barrier, inc=1, device_id={"dp": lax.rem(me + j, peers)}, device_id_type=MESH
        )

    @pl.when(stage < last)
    def _():
        pl.semaphore_signal(barrier, inc=1, device_id={"pipe": stage + 1}, device_id_type=MESH)

    @pl.when(stage > 0)
    def _():
        pl.semaphore_signal(barrier, inc=1, device_id={"pipe": stage - 1}, device_id_type=MESH)

    pl.semaphore_wait(
        barrier, peers - 1 + jnp.minimum(stage, 1) + jnp.minimum(last - stage, 1)
    )

    @pl.when(stage == 0)
    def _():
        for m in range(micro):
            for p, part in enumerate(pieces):
                pltpu.make_async_copy(
                    rows_hbm.at[m, :, part], xbuf.at[m, :, part], x_recv.at[m, p]
                ).start()

    @pl.when(stage == last)
    def _():
        for m in range(micro):
            for p, part in enumerate(pieces):
                pltpu.make_async_copy(
                    cot_hbm.at[m, :, part], ubuf.at[m, :, part], u_recv.at[m, p]
                ).start()

    def cols(c):
        return pl.ds(c * chunk, chunk) if isinstance(c, int) else pl.ds(pl.multiple_of(c * chunk, chunk), chunk)

    def spread_columns(source, target, sems, m):
        for j in range(1, peers):
            peer = lax.rem(me + j, peers)
            pltpu.make_async_remote_copy(
                src_ref=source.at[m, :, pl.ds(pl.multiple_of(peer * share, share), share)],
                dst_ref=target.at[me, m],
                send_sem=sems.at[0],
                recv_sem=sems.at[1],
                device_id={"dp": peer},
                device_id_type=MESH,
            ).start()
        pltpu.make_async_copy(
            source.at[m, :, pl.ds(pl.multiple_of(me * share, share), share)],
            target.at[me, m],
            sems.at[1],
        ).start()

    def spread_whole(source, target, sems, m):
        for j in range(1, peers):
            pltpu.make_async_remote_copy(
                src_ref=source.at[m],
                dst_ref=target.at[me, m],
                send_sem=sems.at[0],
                recv_sem=sems.at[1],
                device_id={"dp": lax.rem(me + j, peers)},
                device_id_type=MESH,
            ).start()
        pltpu.make_async_copy(source.at[m], target.at[me, m], sems.at[1]).start()

    def pass_on(source, target, send, recv, m, p, to):
        return pltpu.make_async_remote_copy(
            src_ref=source.at[m, :, pieces[p]],
            dst_ref=target.at[m, :, pieces[p]],
            send_sem=send.at[m, p],
            recv_sem=recv.at[m, p],
            device_id={"pipe": to},
            device_id_type=MESH,
        )

    def by_piece(run, first, before=None, after=None):
        value = first
        for p in range(PIECES):
            if before is not None:
                before(p)
            for c in range(p * per_piece, (p + 1) * per_piece):
                value = run(c, value)
            if after is not None:
                after(p)
        return value

    def forward(m):
        def square(c, total):
            x = xbuf[m, :, cols(c)].astype(jnp.float32)
            return total + jnp.sum(x * x, axis=-1, keepdims=True)

        total = by_piece(
            square,
            jnp.zeros((rows, 1), jnp.float32),
            before=lambda p: landed(xbuf.at[m, :, pieces[p]], x_recv.at[m, p]),
        )
        inverse = lax.rsqrt(total / width + EPSILON)
        inv_kept[m] = jnp.broadcast_to(inverse, inv_kept.shape[1:])

        def project(c, pre):
            x = xbuf[m, :, cols(c)].astype(jnp.float32)
            n = (x * inverse * gain[:, cols(c)]).astype(jnp.bfloat16)
            normed[m, :, cols(c)] = n
            return pre + jnp.dot(n, w_in[cols(c), :], preferred_element_type=jnp.float32)

        pre = lax.fori_loop(
            0, chunks, project, jnp.zeros((rows, w_in.shape[1]), jnp.float32), unroll=UNROLL
        )
        pre_kept[m] = pre
        hidden = jax.nn.silu(pre).astype(jnp.bfloat16)
        hidden_kept[m] = hidden

        @pl.when(stage < last)
        def _():
            def emit(c, carry):
                x = xbuf[m, :, cols(c)].astype(jnp.float32)
                y = jnp.dot(hidden, w_out[:, cols(c)], preferred_element_type=jnp.float32)
                xsend[m, :, cols(c)] = (x + y).astype(jnp.bfloat16)
                return carry

            by_piece(
                emit,
                0,
                after=lambda p: pass_on(
                    xsend, xbuf, x_sent, x_recv, m, p, stage + 1
                ).start(),
            )

        spread_columns(normed, normed_all, n_sems, m)
        spread_whole(hidden_kept, hidden_all, h_sems, m)

    def backward(m):
        contract = (((1,), (1,)), ((), ()))

        def collect(c, total):
            return total + lax.dot_general(
                ubuf[m, :, cols(c)],
                w_out[:, cols(c)],
                contract,
                preferred_element_type=jnp.float32,
            )

        grad_hidden = by_piece(
            collect,
            jnp.zeros((rows, w_in.shape[1]), jnp.float32),
            before=lambda p: landed(ubuf.at[m, :, pieces[p]], u_recv.at[m, p]),
        )
        spread_columns(ubuf, up_all, p_sems, m)
        pre = pre_kept[m]
        sig = jax.nn.sigmoid(pre)
        grad_pre = (grad_hidden * sig * (1.0 + pre * (1.0 - sig))).astype(jnp.bfloat16)
        grad_kept[m] = grad_pre

        @pl.when(stage > 0)
        def _():
            inverse = inv_kept[m][:, :1]

            mean = jnp.sum(grad_pre.astype(jnp.float32) * pre, axis=-1, keepdims=True) / width

            def emit(c, carry):
                t = lax.dot_general(
                    grad_pre, w_in[cols(c), :], contract, preferred_element_type=jnp.float32
                )
                t = t * gain[:, cols(c)]
                xhat = xbuf[m, :, cols(c)].astype(jnp.float32) * inverse
                u = ubuf[m, :, cols(c)].astype(jnp.float32)
                usend[m, :, cols(c)] = (u + inverse * (t - xhat * mean)).astype(jnp.bfloat16)
                return carry

            by_piece(
                emit,
                0,
                after=lambda p: pass_on(
                    usend, ubuf, u_sent, u_recv, m, p, stage - 1
                ).start(),
            )

        spread_whole(grad_kept, grad_all, g_sems, m)

    delay = jnp.minimum(2 * (last - stage), micro)

    def step(k, carry):
        @pl.when(k < micro)
        def _():
            forward(k)

        @pl.when((k >= delay) & (k < delay + micro))
        def _():
            backward(k - delay)

        return carry

    lax.fori_loop(0, micro + min(2 * last, micro), step, 0)

    for m in range(micro):

        @pl.when(stage < last)
        def _(m=m):
            for p in range(PIECES):
                pass_on(xsend, xbuf, x_sent, x_recv, m, p, stage + 1).wait_send()

        @pl.when(stage > 0)
        def _(m=m):
            for p in range(PIECES):
                pass_on(usend, ubuf, u_sent, u_recv, m, p, stage - 1).wait_send()

    if peers > 1:
        landed(normed_all.at[pl.ds(0, peers - 1)], n_sems.at[0])
        landed(up_all.at[pl.ds(0, peers - 1)], p_sems.at[0])
        landed(hidden_all.at[pl.ds(0, peers - 1)], h_sems.at[0])
        landed(grad_all.at[pl.ds(0, peers - 1)], g_sems.at[0])
    landed(normed_all, n_sems.at[1])
    landed(up_all, p_sems.at[1])
    landed(hidden_all, h_sems.at[1])
    landed(grad_all, g_sems.at[1])


def per_device(sections, peers, inputs, cotangent, plan_order, norm_gain, weight_in, weight_out):
    micro, rows, width = inputs.shape
    inner = weight_in.shape[2]
    share = width // peers
    ordered = jnp.take(inputs, plan_order, axis=0, mode="clip")
    wide, narrow = (micro, rows, width), (micro, rows, inner)
    half, full = jnp.bfloat16, jnp.float32
    dma = pltpu.SemaphoreType.DMA
    anywhere = pl.BlockSpec(memory_space=pl.ANY)
    local = pl.BlockSpec(memory_space=pltpu.VMEM)
    normed_all, up_all, hidden_all, grad_all = pl.pallas_call(
        functools.partial(train_kernel, sections, peers),
        out_shape=(
            jax.ShapeDtypeStruct((peers, micro, rows, share), half),
            jax.ShapeDtypeStruct((peers, micro, rows, share), half),
            jax.ShapeDtypeStruct((peers, micro, rows, inner), half),
            jax.ShapeDtypeStruct((peers, micro, rows, inner), half),
        ),
        in_specs=[anywhere, anywhere, local, local, local],
        out_specs=[anywhere] * 4,
        scratch_shapes=[pltpu.VMEM(wide, half)] * 5
        + [
            pltpu.VMEM(narrow, full),
            pltpu.VMEM(narrow, half),
            pltpu.VMEM(narrow, half),
            pltpu.VMEM((micro, rows, 128), full),
        ]
        + [dma((micro, PIECES))] * 4
        + [dma((2,))] * 4,
        compiler_params=pltpu.CompilerParams(
            collective_id=0, has_side_effects=True, vmem_limit_bytes=60 * 1024 * 1024
        ),
    )(ordered, cotangent, norm_gain, weight_in[0], weight_out[0])
    tokens = peers * micro * rows
    total_in = jnp.einsum(
        "td,tr->dr",
        normed_all.reshape(tokens, share),
        grad_all.reshape(tokens, inner),
        preferred_element_type=full,
    )
    total_out = jnp.einsum(
        "tr,td->rd",
        hidden_all.reshape(tokens, inner),
        up_all.reshape(tokens, share),
        preferred_element_type=full,
    )
    return (total_in.astype(half)[None], total_out.astype(half)[None])


def solution(mesh):
    in_specs = (
        P(None, "dp", None),
        P(None, "dp", None),
        P(),
        P("pipe", None),
        P("pipe", None, None),
        P("pipe", None, None),
    )
    out_specs = (P("pipe", "dp", None), P("pipe", None, "dp"))
    return jax.shard_map(
        functools.partial(per_device, mesh.shape["pipe"], mesh.shape["dp"]),
        mesh=mesh,
        in_specs=in_specs,
        out_specs=out_specs,
        check_vma=False,
    )
```
